512 devices in a mesh: dom: 32 (over x, z), row: 16 (over y, core).
Axes of the slice: x: 4, y: 8, z: 8, core: 2. Of those that a mesh axis runs over, the one named last changes fastest.
Arguments:
- right_side: float32 [131072, 128], P(('dom', 'row')), may hold values from -6 to 6
- spikes: float32 [5, 131072, 512], P(None, ('dom', 'row')), may hold values from -0.1875 to 0.1875
- inverses: float32 [32, 1024, 1024], P('dom', 'row'), may hold values from -1 to 2
Outputs:
- solution: float32 [131072, 128], P(('dom', 'row'))
The draws below stay inside these ranges and needn't reach their ends.
All inputs are finite; a program needn't handle non-finite values.
Results may differ from the reference program's by a relative error of at most 0.0001.
Values sent between devices are 32-bit elements; how exact they have to be, the bound alone decides.
No kernel may reach another device: no remote copies, remote signals or barrier semaphores. Data moves between devices by JAX's collectives and lax.ppermute only.
A program may use at most 64 MiB of HBM per device.

```python
import math
import jax
import jax.numpy as jnp
from jax import lax

K = 512
NRHS = 128
PARTITIONS = 32
LEVELS = 5
ROWS = 131072


def draw_inverses(key, part):
    order = 2 * K
    spread_size = 0.5 / math.sqrt(order)
    bound_value = spread_size * math.sqrt(3.0)
    offsets = jax.random.uniform(key, (PARTITIONS, order, order), jnp.float32, -bound_value, bound_value)
    return offsets + jnp.eye(order, dtype=jnp.float32)[None]


def block_levels(own_key, extent, cuts, least, largest):
    gain = 1.0
    for position, blocks in cuts:
        heights = jax.random.uniform(jax.random.fold_in(jax.random.fold_in(own_key, 6), position), (blocks,), jnp.float32, least / len(cuts), largest / len(cuts))
        gain = gain * jnp.repeat(jnp.exp(heights), extent[position] // blocks).reshape((-1,) + (1,) * (len(extent) - 1 - position))
    return gain


def normal_values(key, shape, width, reach, pieces=(), kind=jnp.bfloat16):
    gain = block_levels(key, shape, pieces, -0.22, 0.18) if pieces else 1.0
    drawn = jax.random.normal(key, shape, jnp.float32) * width * gain
    return jnp.minimum(jnp.maximum(drawn, -reach), reach).astype(kind)


def setup_inputs(seed: int = 0) -> dict:
    arg_keys = jax.random.split(jax.random.key(seed), 4)
    return {
        "right_side": normal_values(arg_keys[0], (ROWS, NRHS), 1.0, 6.0, ((0, 512),), jnp.float32),
        "spikes": normal_values(arg_keys[1], (LEVELS, ROWS, K), (2 * K) ** -0.5, 0.1875, ((1, 512),), jnp.float32),
        "inverses": draw_inverses(jax.random.fold_in(arg_keys[3], 71), 0),
    }


exact_mode = lax.Precision.HIGHEST


def reference(right_side, spikes, inverses):
    total_rows, columns = right_side.shape
    spike_cols = spikes.shape[2]
    part_rows = total_rows // PARTITIONS
    current = right_side
    for level_at in range(LEVELS):
        half_group = 2 ** level_at
        block_rows = half_group * part_rows
        groups = PARTITIONS // (2 * half_group)
        shaped = current.reshape(groups, 2, block_rows, columns)
        tip_rows = jnp.concatenate([shaped[:, 0, block_rows - spike_cols:], shaped[:, 1, :spike_cols]], axis=1)
        owners = (jnp.arange(groups) * 2 * half_group + half_group).astype(jnp.int32)
        matrices = jnp.take(inverses, owners, axis=0)
        solved = jnp.einsum("gij,gjm->gim", matrices, tip_rows, precision=exact_mode)
        spike_rows = spikes[level_at].reshape(groups, 2, block_rows, spike_cols)
        left_term = jnp.einsum("gbk,gkm->gbm", spike_rows[:, 0], solved[:, spike_cols:], precision=exact_mode)
        right_term = jnp.einsum("gbk,gkm->gbm", spike_rows[:, 1], solved[:, :spike_cols], precision=exact_mode)
        shaped = shaped - jnp.stack([left_term, right_term], axis=1)
        current = shaped.reshape(total_rows, columns)
    return current
```

```python
import jax
import jax.numpy as jnp
from jax import lax
from jax.sharding import Mesh
from jax.sharding import PartitionSpec as P

CHIPS, CORES = 8, 2
AXES = ("dom", "y", "c")
MODE = lax.Precision.HIGH


def flat(dom, y, c):
    return (dom * CHIPS + y) * CORES + c


def both_cores(links):
    return [(flat(*a, c), flat(*b, c)) for a, b in links for c in range(CORES)]


def permute(value, pairs):
    return lax.ppermute(value, AXES, pairs)


def dot(a, b):
    return jnp.dot(a, b, precision=MODE, preferred_element_type=jnp.float32)


def cores_gather(value):
    return lax.all_gather(value, "c", axis=0, tiled=True)


def boundaries(parts, level):
    return range(1 << level, parts, 2 << level)


def upper(p):
    return (p, 0)


def lower(p):
    return (p - 1, CHIPS - 1)


def inverse_pairs(parts, j):
    pairs = []
    for p in range(1, parts):
        for c in range(CORES):
            for chip, base in ((upper(p), 0), (lower(p), CHIPS)):
                r = base + (CHIPS // CORES) * c + j
                pairs.append((flat(p, r // CORES, r % CORES), flat(*chip, c)))
    return pairs


def partner_links(parts, step):
    links = []
    for p in range(step, parts, step):
        links += [(upper(p), lower(p)), (lower(p), upper(p))]
    return links


def cross_links(parts, level):
    s = 1 << level
    links = []
    for p in boundaries(parts, level):
        links += [(upper(p), (p + s - 1, CHIPS - 1)), (lower(p), (p - s, 0))]
    return links


def along_links(parts, level):
    s = 1 << level
    links = []
    for p in boundaries(parts, level):
        if p + s < parts:
            links.append((upper(p), upper(p + s)))
        if p - s > 0:
            links.append((lower(p), lower(p - s)))
    return links


def spread_stages(level):
    s = 1 << level
    last = CHIPS - 1
    stages = []
    steps = [1 << b for b in range(level - 1, -1, -1)]
    if level < 4:
        low, high = {0}, {s - 1}
        for step in steps:
            links = [((d, 0), (d + step, 0)) for d in sorted(low)]
            links += [((d, last), (d - step, last)) for d in sorted(high)]
            low |= {d + step for d in low}
            high |= {d - step for d in high}
            stages.append(links)
    else:
        stages.append([((0, 0), (0, last))])
        low = {0}
        for step in steps:
            stages.append([((d, y), (d + step, y)) for d in sorted(low) for y in (0, last)])
            low |= {d + step for d in low}
    stages.append([((d, a), (d, b)) for d in range(s) for a, b in ((0, 2), (last, last - 2))])
    stages.append(
        [((d, a), (d, b)) for d in range(s) for a, b in ((0, 1), (2, 3), (last, last - 1), (last - 2, last - 3))]
    )
    return stages


def placed(parts, level, links):
    out = []
    for p in boundaries(parts, level):
        for (d, y), (e, w) in links:
            out.append(((p + d, y), (p + e, w)))
            out.append(((p - 1 - d, CHIPS - 1 - y), (p - 1 - e, CHIPS - 1 - w)))
    return out


class Marks:
    def __init__(self, count):
        self.words = [0] * count
        self.bits = 0

    def add(self, links):
        for _, b in links:
            for c in range(CORES):
                self.words[flat(*b, c)] |= 1 << self.bits
        self.bits += 1
        return self.bits - 1


def body(right_side, spikes, inverses):
    parts = lax.axis_size("dom")
    levels, rows, cols = spikes.shape
    me = flat(lax.axis_index("dom"), lax.axis_index("y"), lax.axis_index("c"))
    inverse = inverses[0]

    marks = Marks(parts * CHIPS * CORES)
    trees = []
    for level in range(levels):
        tree = []
        if level < levels - 1:
            links = cross_links(parts, level)
            tree.append((None, marks.add(links)))
        for stage in spread_stages(level):
            links = placed(parts, level, stage)
            tree.append((both_cores(links), marks.add(links)))
        trees.append(tree)
    word = lax.dynamic_index_in_dim(jnp.array(marks.words, jnp.uint32), me, 0, keepdims=False)

    def marked(bit):
        return (word >> bit) & 1 == 1

    b0, b1, t0, t1 = jnp.split(inverse, 4, axis=1)
    for_upper = lax.axis_index("y") < CHIPS // 2
    first, second = jnp.where(for_upper, t0, b0), jnp.where(for_upper, b0, t0)
    third, fourth = jnp.where(for_upper, t1, b1), jnp.where(for_upper, b1, t1)
    arranged = jnp.concatenate([first, second, third, fourth], axis=1)
    own = right_side
    other = permute(own, both_cores(partner_links(parts, 1)))
    pieces = [permute(arranged, inverse_pairs(parts, j)) for j in range(CHIPS // CORES)]
    matrix = jnp.concatenate(pieces, axis=0)
    other_spikes = [
        permute(spikes[level], both_cores(partner_links(parts, 2 << level))) for level in range(levels - 1)
    ]

    out = right_side
    for level in range(levels):
        tips = cores_gather(jnp.concatenate([own, other], axis=0))
        solved = dot(matrix, tips)
        held = solved
        tree = trees[level]
        if level < levels - 1:
            crossed = permute(solved, both_cores(cross_links(parts, level)))
            along = permute(solved, both_cores(along_links(parts, level)))
            own = own - dot(spikes[level], cores_gather(crossed))
            other = other - dot(other_spikes[level], cores_gather(along))
            held = jnp.where(marked(tree[0][1]), crossed, held)
            tree = tree[1:]
        for pairs, bit in tree:
            held = jnp.where(marked(bit), permute(held, pairs), held)
        out = out - dot(spikes[level], cores_gather(held))
    return out


def solution(mesh):
    fine = Mesh(mesh.devices.reshape(mesh.shape["dom"], CHIPS, CORES), AXES)
    rows = ("dom", "y", "c")
    in_specs = (P(rows, None), P(None, rows, None), P("dom", ("y", "c"), None))
    return jax.shard_map(body, mesh=fine, in_specs=in_specs, out_specs=P(rows, None), check_vma=False)
```

```python
import jax
import jax.numpy as jnp
from jax import lax
from jax.sharding import Mesh
from jax.sharding import PartitionSpec as P


CHIPS, CORES, RING = 8, 2, 8
LAST = CHIPS - 1
AXES = ("dom", "y", "c")
MODE = lax.Precision.HIGH


def flat(dom, y, c):
    return (dom * CHIPS + y) * CORES + c


def both_cores(links):
    return [(flat(*a, c), flat(*b, c)) for a, b in links for c in range(CORES)]


def permute(value, links):
    return lax.ppermute(value, AXES, both_cores(links))


def swap_cores(value):
    return lax.ppermute(value, "c", [(0, 1), (1, 0)])


def cores_gather(value):
    return lax.all_gather(value, "c", axis=0, tiled=True)


def dot_t(a, b):
    return lax.dot_general(a, b, (((1,), (1,)), ((), ())), precision=MODE, preferred_element_type=jnp.float32)


def boundaries(parts, level):
    return range(1 << level, parts, 2 << level)


def upper(p):
    return (p, 0)


def lower(p):
    return (p - 1, LAST)


def inverse_links(parts, j):
    links = []
    for p in range(1, parts):
        links += [((p, j), upper(p)), ((p, (j + CHIPS // 2) % CHIPS), lower(p))]
    return links


def cross_links(parts, level):
    s = 1 << level
    links = []
    for p in boundaries(parts, level):
        links += [(upper(p), (p + s - 1, LAST)), (lower(p), (p - s, 0))]
    return links


def along_links(parts, level):
    s = 1 << level
    links = []
    for p in boundaries(parts, level):
        links += [(upper(p), (p - s, 0)), (lower(p), (p + s - 1, LAST))]
    return links


def partner_links(parts, step):
    links = []
    for p in range(step, parts, step):
        links += [(upper(p), lower(p)), (lower(p), upper(p))]
    return links


def corner_links(parts, bit):
    step = 1 << bit
    low = 2 * step - 1
    links = []
    for q in range(parts):
        if q & low == low:
            links.append(((q, LAST), (q - step, LAST)))
        if q & low == 0:
            links.append(((q, 0), (q + step, 0)))
    return links


def top_links(parts, moves):
    p = parts // 2
    links = []
    for a, b in moves:
        links += [((p + a, 0), (p + b, 0)), ((p - 1 - a, LAST), (p - 1 - b, LAST))]
    return links


def chip_links(parts, pairs):
    return [((q, a), (q, b)) for q in range(parts) for a, b in pairs]


ENDS = ((0, LAST), (LAST, 0))
INNER = ((0, 2), (LAST, LAST - 2))
REST = ((0, 1), (2, 3), (LAST, LAST - 1), (LAST - 2, LAST - 3))


def body(right_side, spikes, inverses):
    parts = lax.axis_size("dom")
    levels, _, cols = spikes.shape
    top = levels - 1
    first_core = lax.axis_index("c") == 0
    mine = lax.axis_index("c") * (right_side.shape[1] // CORES)

    inverse = inverses[0]
    below, above = inverse[:, :cols], inverse[:, cols:]
    for_upper = lax.axis_index("y") < CHIPS // 2
    sent = jnp.where(for_upper, above, below), jnp.where(for_upper, below, above)
    pieces = [permute(sent[j // (CHIPS // 2)], inverse_links(parts, j)) for j in range(CHIPS)]
    blocks = []
    for j in range(0, CHIPS, 2):
        gathered = cores_gather(jnp.concatenate(pieces[j : j + 2], axis=0))
        blocks += [jnp.split(gathered, 4, axis=0)[i] for i in (0, 2, 1, 3)]
    stay, go = jnp.concatenate(blocks[:CHIPS], axis=0), jnp.concatenate(blocks[CHIPS:], axis=0)

    both = cores_gather(right_side)
    own = lax.dynamic_slice_in_dim(both.T, mine, right_side.shape[1] // CORES, 0)
    here, there = spikes, swap_cores(spikes)
    tip_spikes = [
        jnp.concatenate(
            [jnp.where(first_core, here[k], there[k]), jnp.where(first_core, there[k], here[k])], axis=0
        )
        for k in range(top)
    ]

    held = []
    for level in range(levels):
        near = dot_t(own, stay)
        if level == top:
            far = dot_t(own, go)
            break
        solved = permute(near, cross_links(parts, level))
        far = dot_t(own, go)
        solved = solved + permute(far, along_links(parts, level))
        own = own - dot_t(solved, tip_spikes[level])
        held.append(solved)

    def spread_chips(value):
        for pairs in (ENDS, INNER, REST):
            value = value + permute(value, chip_links(parts, pairs))
        return value

    width = solved.shape[0]
    moved = held[1] + permute(held[1], corner_links(parts, 0))
    low = spread_chips(jnp.concatenate([held[0], moved], axis=0))
    third = held[3] + permute(held[3], corner_links(parts, 2))
    third = jnp.concatenate([held[2], third], axis=0)
    for bit in (1, 0):
        third = third + permute(third, corner_links(parts, bit))

    p = parts // 2
    at_root = (lax.axis_index("y") == 0) & (lax.axis_index("dom") == p)
    at_root |= (lax.axis_index("y") == LAST) & (lax.axis_index("dom") == p - 1)
    solved = jnp.where(at_root, near, 0.0) + permute(far, partner_links(parts, p))
    last = solved + permute(solved, top_links(parts, [(0, RING)]))
    lines = range(0, p, RING)
    for k, (starts, ends) in enumerate(((((0, 3), (0, 5)), ()), (((0, 1), (3, 4), (5, 6)), ((0, 7), (3, 2))))):
        if k == 0:
            sets = [[starts[0]], [starts[1]]]
        else:
            sets = [starts, ends]
        got = [permute(last, top_links(parts, [(n + a, n + b) for n in lines for a, b in moves])) for moves in sets]
        last = last + got[0] + got[1]
    pair = spread_chips(jnp.concatenate([third, last], axis=0))

    def spread_update(out, level, full):
        return out - lax.dot_general(
            spikes[level], full, (((1,), (1,)), ((), ())), precision=MODE, preferred_element_type=jnp.float32
        )

    out = right_side
    for value, first in ((low, 0), (pair, 2)):
        count = value.shape[0] // width
        ends = cores_gather(value)
        for k in range(count):
            full = jnp.concatenate([ends[i * width : (i + 1) * width] for i in (k, k + count)], axis=0)
            out = spread_update(out, first + k, full)
    return out


def solution(mesh):
    fine = Mesh(mesh.devices.reshape(mesh.shape["dom"], CHIPS, CORES), AXES)
    rows = ("dom", "y", "c")
    in_specs = (P(rows, None), P(None, rows, None), P("dom", ("y", "c"), None))

    return jax.shard_map(body, mesh=fine, in_specs=in_specs, out_specs=P(rows, None), check_vma=False)
```

```python
import jax
import jax.numpy as jnp
from jax import lax
from jax.sharding import Mesh
from jax.sharding import PartitionSpec as P


CHIPS, CORES, RING = 8, 2, 8
LAST = CHIPS - 1
AXES = ("dom", "y", "c")
MODE = lax.Precision.HIGH


def flat(dom, y, c):
    return (dom * CHIPS + y) * CORES + c


def both_cores(links):
    return [(flat(*a, c), flat(*b, c)) for a, b in links for c in range(CORES)]


def permute(value, links):
    return lax.ppermute(value, AXES, both_cores(links))


def swap_cores(value):
    return lax.ppermute(value, "c", [(0, 1), (1, 0)])


def cores_gather(value):
    return lax.all_gather(value, "c", axis=0, tiled=True)


def dot_t(a, b):
    return lax.dot_general(a, b, (((1,), (1,)), ((), ())), precision=MODE, preferred_element_type=jnp.float32)


def boundaries(parts, level):
    return range(1 << level, parts, 2 << level)


def upper(p):
    return (p, 0)


def lower(p):
    return (p - 1, LAST)


def inverse_links(parts, j):
    links = []
    for p in range(1, parts):
        links += [((p, j), upper(p)), ((p, (j + CHIPS // 2) % CHIPS), lower(p))]
    return links


def cross_links(parts, level):
    s = 1 << level
    links = []
    for p in boundaries(parts, level):
        links += [(upper(p), (p + s - 1, LAST)), (lower(p), (p - s, 0))]
    return links


def along_links(parts, level):
    s = 1 << level
    links = []
    for p in boundaries(parts, level):
        links += [(upper(p), (p - s, 0)), (lower(p), (p + s - 1, LAST))]
    return links


def corner_links(parts, bit):
    step = 1 << bit
    low = 2 * step - 1
    links = []
    for q in range(parts):
        if q & low == low:
            links.append(((q, LAST), (q - step, LAST)))
        if q & low == 0:
            links.append(((q, 0), (q + step, 0)))
    return links


def top_links(parts, moves):
    p = parts // 2
    links = []
    for (a, y), (b, w) in moves:
        links += [((p + a, y), (p + b, w)), ((p - 1 - a, LAST - y), (p - 1 - b, LAST - w))]
    return links


def line_links(parts, moves):
    lines = [(n, y) for n in range(0, parts // 2, RING) for y in (0, LAST)]
    return top_links(parts, [((n + a, y), (n + b, y)) for n, y in lines for a, b in moves])


def chip_links(parts, pairs):
    return [((q, a), (q, b)) for q in range(parts) for a, b in pairs]


ENDS = ((0, LAST), (LAST, 0))
INNER = ((0, 2), (LAST, LAST - 2))
REST = ((0, 1), (2, 3), (LAST, LAST - 1), (LAST - 2, LAST - 3))


def body(right_side, spikes, inverses):
    parts = lax.axis_size("dom")
    levels, _, cols = spikes.shape
    top = levels - 1
    first_core = lax.axis_index("c") == 0
    mine = lax.axis_index("c") * (right_side.shape[1] // CORES)

    inverse = inverses[0]
    below, above = inverse[:, :cols], inverse[:, cols:]
    for_upper = lax.axis_index("y") < CHIPS // 2
    sent = jnp.where(for_upper, above, below), jnp.where(for_upper, below, above)
    pieces = [permute(sent[j // (CHIPS // 2)], inverse_links(parts, j)) for j in range(CHIPS)]
    blocks = []
    for j in range(0, CHIPS, 2):
        gathered = cores_gather(jnp.concatenate(pieces[j : j + 2], axis=0))
        blocks += [jnp.split(gathered, 4, axis=0)[i] for i in (0, 2, 1, 3)]
    stay, go = jnp.concatenate(blocks[:CHIPS], axis=0), jnp.concatenate(blocks[CHIPS:], axis=0)

    both = cores_gather(right_side)
    own = lax.dynamic_slice_in_dim(both.T, mine, right_side.shape[1] // CORES, 0)
    here, there = spikes, swap_cores(spikes)
    tip_spikes = [
        jnp.concatenate([jnp.where(first_core, here[k], there[k]), jnp.where(first_core, there[k], here[k])], axis=0)
        for k in range(top)
    ]

    held = []
    for level in range(levels):
        if level < top:
            links = cross_links(parts, level), along_links(parts, level)
        else:
            p = parts // 2
            links = (
                [(upper(p), (p, LAST)), (lower(p), (p - 1, 0))],
                [(upper(p), (p - 1, 0)), (lower(p), (p, LAST))],
            )
        solved = permute(dot_t(own, stay), links[0])
        solved = solved + permute(dot_t(own, go), links[1])
        held.append(solved)
        if level < top:
            own = own - dot_t(solved, tip_spikes[level])

    def spread_chips(value):
        for pairs in (INNER, REST):
            value = value + permute(value, chip_links(parts, pairs))
        return value

    def spread_ends(value):
        return value + permute(value, chip_links(parts, ENDS))

    width = solved.shape[0]
    moved = held[1] + permute(held[1], corner_links(parts, 0))
    low = spread_chips(spread_ends(jnp.concatenate([held[0], moved], axis=0)))
    third = held[3] + permute(held[3], corner_links(parts, 2))
    third = jnp.concatenate([held[2], third], axis=0)
    for bit in (1, 0):
        third = third + permute(third, corner_links(parts, bit))

    third = spread_ends(third)

    last = held[top]
    root = (0, LAST)
    got = [permute(last, top_links(parts, [(root, to)])) for to in ((RING, 0), (RING, LAST), (0, 0))]
    last = last + got[0] + got[1] + got[2]
    for ups, downs in ((((0, 3),), ((0, 5),)), (((0, 1), (3, 4), (5, 6)), ((0, 7), (3, 2)))):
        up = permute(last, line_links(parts, ups))
        last = last + up + permute(last, line_links(parts, downs))
    pair = spread_chips(jnp.concatenate([third, last], axis=0))

    def spread_update(out, level, full):
        return out - lax.dot_general(
            spikes[level], full, (((1,), (1,)), ((), ())), precision=MODE, preferred_element_type=jnp.float32
        )

    out = right_side
    for value, first in ((low, 0), (pair, 2)):
        count = value.shape[0] // width
        ends = cores_gather(value)
        for k in range(count):
            full = jnp.concatenate([ends[i * width : (i + 1) * width] for i in (k, k + count)], axis=0)
            out = spread_update(out, first + k, full)
    return out


def solution(mesh):
    fine = Mesh(mesh.devices.reshape(mesh.shape["dom"], CHIPS, CORES), AXES)
    rows = ("dom", "y", "c")
    in_specs = (P(rows, None), P(None, rows, None), P("dom", ("y", "c"), None))

    return jax.shard_map(body, mesh=fine, in_specs=in_specs, out_specs=P(rows, None), check_vma=False)
```

```python
import jax
import jax.numpy as jnp
from jax import lax
from jax.sharding import Mesh
from jax.sharding import PartitionSpec as P


CHIPS, CORES, RING = 8, 2, 8
LAST = CHIPS - 1
AXES = ("dom", "y", "c")
MODE = lax.Precision.HIGH


def flat(dom, y, c):
    return (dom * CHIPS + y) * CORES + c


def both_cores(links):
    return [(flat(*a, c), flat(*b, c)) for a, b in links for c in range(CORES)]


def permute(value, links):
    return lax.ppermute(value, AXES, both_cores(links))


def swap_cores(value):
    return lax.ppermute(value, "c", [(0, 1), (1, 0)])


def cores_gather(value):
    return lax.all_gather(value, "c", axis=0, tiled=True)


def split(value):
    high = lax.reduce_precision(value, 8, 7)
    return high.astype(jnp.bfloat16), (value - high).astype(jnp.bfloat16)


def split_matrix(value):
    high, low = split(value)
    return jnp.concatenate([high, high, low], axis=1)


def dot_split(value, matrix):
    high, low = split(value)
    wide = jnp.concatenate([high, low, high], axis=1)
    return lax.dot_general(wide, matrix, (((1,), (1,)), ((), ())), preferred_element_type=jnp.float32)


def boundaries(parts, level):
    return range(1 << level, parts, 2 << level)


def upper(p):
    return (p, 0)


def lower(p):
    return (p - 1, LAST)


RELAYED = (3, 4, 5, 6)
ARRIVAL = (3, 4, 5, 6, 0, 1, 2, 7)


def relay_links(parts):
    return [((p, m), (p - 1, m)) for p in range(1, parts) for m in RELAYED]


def inverse_links(parts, j):
    m = (j + CHIPS // 2) % CHIPS
    links = []
    for p in range(1, parts):
        links += [((p, j), upper(p)), ((p - 1 if m in RELAYED else p, m), lower(p))]
    return links


def cross_links(parts, level):
    s = 1 << level
    links = []
    for p in boundaries(parts, level):
        links += [(upper(p), (p + s - 1, LAST)), (lower(p), (p - s, 0))]
    return links


def along_links(parts, level):
    s = 1 << level
    links = []
    for p in boundaries(parts, level):
        links += [(upper(p), (p - s, 0)), (lower(p), (p + s - 1, LAST))]
    return links


def halving_links(parts, level, bit):
    step = 1 << bit
    low = 2 * step - 1
    links = []
    for q in range(parts):
        for y in (0, LAST):
            if q >> level & 1 and q & low == low:
                links.append(((q, y), (q - step, y)))
            if not q >> level & 1 and q & low == 0:
                links.append(((q, y), (q + step, y)))
    return links


def neighbour_links(parts):
    return [((q, y), (q ^ 1, y)) for q in range(parts) for y in (0, LAST)]


def ring_links(moves, roots):
    links = []
    for n, from_last in enumerate(roots):
        for a, b in moves:
            if from_last:
                a, b = RING - 1 - a, RING - 1 - b
            links += [((RING * n + a, y), (RING * n + b, y)) for y in (0, LAST)]
    return links


def top_links(parts, moves):
    p = parts // 2
    links = []
    for (a, y), (b, w) in moves:
        links += [((p + a, y), (p + b, w)), ((p - 1 - a, LAST - y), (p - 1 - b, LAST - w))]
    return links


def chip_links(parts, pairs):
    return [((q, a), (q, b)) for q in range(parts) for a, b in pairs]


ENDS = ((0, LAST), (LAST, 0))
INNER = ((0, 2), (LAST, LAST - 2))
REST = ((0, 1), (2, 3), (LAST, LAST - 1), (LAST - 2, LAST - 3))


def body(right_side, spikes, inverses):
    parts = lax.axis_size("dom")
    levels, _, cols = spikes.shape
    top = levels - 1
    first_core = lax.axis_index("c") == 0
    mine = lax.axis_index("c") * (right_side.shape[1] // CORES)

    inverse = inverses[0]
    below, above = inverse[:, :cols], inverse[:, cols:]
    chip = lax.axis_index("y")
    direct = (chip >= RELAYED[0]) & (chip <= RELAYED[-1])
    relayed = permute(below, relay_links(parts))
    sent = jnp.where(direct, above, below), jnp.where(direct, relayed, above)
    pieces = [permute(sent[n // (CHIPS // 2)], inverse_links(parts, j)) for n, j in enumerate(ARRIVAL)]
    blocks = [None] * (2 * CHIPS)
    for n in range(0, CHIPS, 2):
        gathered = cores_gather(jnp.concatenate(pieces[n : n + 2], axis=0))
        for i, block in enumerate(jnp.split(gathered, 4, axis=0)):
            blocks[2 * ARRIVAL[n + i % 2] + i // 2] = block
    stay, go = (split_matrix(jnp.concatenate(half, axis=0)) for half in (blocks[:CHIPS], blocks[CHIPS:]))

    both = cores_gather(right_side)
    own = lax.dynamic_slice_in_dim(both.T, mine, right_side.shape[1] // CORES, 0)
    here, there = spikes, swap_cores(spikes)
    tip_spikes = [
        split_matrix(
            jnp.concatenate(
                [jnp.where(first_core, here[k], there[k]), jnp.where(first_core, there[k], here[k])], axis=0
            )
        )
        for k in range(top)
    ]

    held = []
    for level in range(levels):
        if level < top:
            links = cross_links(parts, level), along_links(parts, level)
        else:
            p = parts // 2
            links = (
                [(upper(p), (p, LAST)), (lower(p), (p - 1, 0))],
                [(upper(p), (p - 1, 0)), (lower(p), (p, LAST))],
            )
        solved = permute(dot_split(own, stay), links[0])
        leaving = dot_split(own, go)
        solved = solved + permute(leaving, links[1])
        held.append(lax.optimization_barrier(solved))
        if level < top:
            change = dot_split(solved, tip_spikes[level])
            own = own - change

    def spread_chips(value):
        for pairs in (INNER, REST):
            value = value + permute(value, chip_links(parts, pairs))
        return value

    def spread_ends(value):
        return value + permute(value, chip_links(parts, ENDS))

    def spread_rings(value, roots):
        rounds = ((((0, 3),), ((0, 5),)), (((0, 1), (3, 4), (5, 6)), ((0, 7), (3, 2))))
        for ups, downs in rounds:
            up = permute(value, ring_links(ups, roots))
            value = value + up + permute(value, ring_links(downs, roots))
        return value

    width = solved.shape[0]
    low = spread_ends(jnp.concatenate(held[:2], axis=0))
    first = low[width:]
    first = first + permute(first, neighbour_links(parts))
    low = spread_chips(jnp.concatenate([low[:width], first], axis=0))
    second = spread_ends(held[2])
    second = second + permute(second, halving_links(parts, 2, 1))
    second = second + permute(second, neighbour_links(parts))
    third = spread_ends(held[3])
    for bit in (2, 1):
        third = third + permute(third, halving_links(parts, 3, bit))
    third = third + permute(third, neighbour_links(parts))
    pair = jnp.concatenate([second, third], axis=0)

    last = held[top]
    got = [permute(last, top_links(parts, [((0, LAST), to)])) for to in ((RING, 0), (RING, LAST), (0, 0))]
    last = spread_rings(last + got[0] + got[1] + got[2], (True, True, False, False))
    pair = spread_chips(jnp.concatenate([pair, last], axis=0))

    def spread_update(out, level, full):
        return out - lax.dot_general(
            spikes[level], full, (((1,), (1,)), ((), ())), precision=MODE, preferred_element_type=jnp.float32
        )

    out = right_side
    for value, first in ((low, 0), (pair, 2)):
        count = value.shape[0] // width
        ends = cores_gather(value)
        for k in range(count):
            full = jnp.concatenate([ends[i * width : (i + 1) * width] for i in (k, k + count)], axis=0)
            out = spread_update(out, first + k, full)
    return out


def solution(mesh):
    fine = Mesh(mesh.devices.reshape(mesh.shape["dom"], CHIPS, CORES), AXES)
    rows = ("dom", "y", "c")
    in_specs = (P(rows, None), P(None, rows, None), P("dom", ("y", "c"), None))

    return jax.shard_map(body, mesh=fine, in_specs=in_specs, out_specs=P(rows, None), check_vma=False)
```

```python
import jax
import jax.numpy as jnp
from jax import lax
from jax.sharding import Mesh
from jax.sharding import PartitionSpec as P


CHIPS, CORES, RING = 8, 2, 8
LAST = CHIPS - 1
AXES = ("dom", "y", "c")
MODE = lax.Precision.HIGH


def flat(dom, y, c):
    return (dom * CHIPS + y) * CORES + c


def both_cores(links):
    return [(flat(*a, c), flat(*b, c)) for a, b in links for c in range(CORES)]


def permute(value, links):
    return lax.ppermute(value, AXES, both_cores(links))


def swap_cores(value):
    return lax.ppermute(value, "c", [(0, 1), (1, 0)])


def cores_gather(value):
    return lax.all_gather(value, "c", axis=0, tiled=True)


def split(value):
    high = lax.reduce_precision(value, 8, 7)
    return high.astype(jnp.bfloat16), (value - high).astype(jnp.bfloat16)


def split_matrix(value):
    high, low = split(value)
    return jnp.concatenate([high, high, low], axis=1)


def dot_split(value, matrix):
    high, low = split(value)
    wide = jnp.concatenate([high, low, high], axis=1)
    return lax.dot_general(wide, matrix, (((1,), (1,)), ((), ())), preferred_element_type=jnp.float32)


def boundaries(parts, level):
    return range(1 << level, parts, 2 << level)


def upper(p):
    return (p, 0)


def lower(p):
    return (p - 1, LAST)


RELAYED = (3, 4, 5, 6)
ARRIVAL = (3, 4, 5, 6, 0, 1, 2, 7)


def relay_links(parts):
    return [((p, m), (p - 1, m)) for p in range(1, parts) for m in RELAYED]


def inverse_links(parts, j):
    m = (j + CHIPS // 2) % CHIPS
    links = []
    for p in range(1, parts):
        links += [((p, j), upper(p)), ((p - 1 if m in RELAYED else p, m), lower(p))]
    return links


def cross_links(parts, level):
    s = 1 << level
    links = []
    for p in boundaries(parts, level):
        links += [(upper(p), (p + s - 1, LAST)), (lower(p), (p - s, 0))]
    return links


def along_links(parts, level):
    s = 1 << level
    links = []
    for p in boundaries(parts, level):
        links += [(upper(p), (p - s, 0)), (lower(p), (p + s - 1, LAST))]
    return links


def halving_links(parts, level, bit):
    step = 1 << bit
    low = 2 * step - 1
    links = []
    for q in range(parts):
        for y in (0, LAST):
            if q >> level & 1 and q & low == low:
                links.append(((q, y), (q - step, y)))
            if not q >> level & 1 and q & low == 0:
                links.append(((q, y), (q + step, y)))
    return links


def neighbour_links(parts):
    return [((q, y), (q ^ 1, y)) for q in range(parts) for y in (0, LAST)]


def ring_links(moves, roots):
    links = []
    for n, from_last in enumerate(roots):
        for a, b in moves:
            if from_last:
                a, b = RING - 1 - a, RING - 1 - b
            links += [((RING * n + a, y), (RING * n + b, y)) for y in (0, LAST)]
    return links


def top_links(parts, moves):
    p = parts // 2
    links = []
    for (a, y), (b, w) in moves:
        links += [((p + a, y), (p + b, w)), ((p - 1 - a, LAST - y), (p - 1 - b, LAST - w))]
    return links


def chip_links(parts, pairs):
    return [((q, a), (q, b)) for q in range(parts) for a, b in pairs]


ENDS = ((0, LAST), (LAST, 0))
INNER = ((0, 2), (LAST, LAST - 2))
REST = ((0, 1), (2, 3), (LAST, LAST - 1), (LAST - 2, LAST - 3))


def body(right_side, spikes, inverses):
    parts = lax.axis_size("dom")
    levels, _, cols = spikes.shape
    top = levels - 1
    first_core = lax.axis_index("c") == 0
    mine = lax.axis_index("c") * (right_side.shape[1] // CORES)

    inverse = inverses[0]
    below, above = inverse[:, :cols], inverse[:, cols:]
    chip = lax.axis_index("y")
    direct = (chip >= RELAYED[0]) & (chip <= RELAYED[-1])
    relayed = permute(below, relay_links(parts))
    sent = jnp.where(direct, above, below), jnp.where(direct, relayed, above)
    pieces = [permute(sent[n // (CHIPS // 2)], inverse_links(parts, j)) for n, j in enumerate(ARRIVAL)]
    blocks = [None] * (2 * CHIPS)
    for n in range(0, CHIPS, 2):
        gathered = cores_gather(jnp.concatenate(pieces[n : n + 2], axis=0))
        for i, block in enumerate(jnp.split(gathered, 4, axis=0)):
            blocks[2 * ARRIVAL[n + i % 2] + i // 2] = block
    stay, go = (split_matrix(jnp.concatenate(half, axis=0)) for half in (blocks[:CHIPS], blocks[CHIPS:]))

    both = cores_gather(right_side)
    own = lax.dynamic_slice_in_dim(both.T, mine, right_side.shape[1] // CORES, 0)
    here, there = spikes, swap_cores(spikes)
    tip_spikes = [
        split_matrix(
            jnp.concatenate(
                [jnp.where(first_core, here[k], there[k]), jnp.where(first_core, there[k], here[k])], axis=0
            )
        )
        for k in range(top)
    ]

    held = []
    for level in range(levels):
        if level < top:
            links = cross_links(parts, level), along_links(parts, level)
        else:
            p = parts // 2
            links = (
                [(upper(p), (p, LAST)), (lower(p), (p - 1, 0))],
                [(upper(p), (p - 1, 0)), (lower(p), (p, LAST))],
            )
        solved = permute(dot_split(own, stay), links[0])
        leaving = dot_split(own, go)
        solved = solved + permute(leaving, links[1])
        held.append(lax.optimization_barrier(solved))
        if level < top:
            change = dot_split(solved, tip_spikes[level])
            own = own - change

    def spread_chips(value):
        for pairs in (INNER, REST):
            got = permute(value, chip_links(parts, pairs))
            value = value + got
        return value

    def spread_ends(value):
        return value + permute(value, chip_links(parts, ENDS))

    def spread_rings(value, roots):
        rounds = ((((0, 3),), ((0, 5),)), (((0, 1), (3, 4), (5, 6)), ((0, 7), (3, 2))))
        for ups, downs in rounds:
            up = permute(value, ring_links(ups, roots))
            down = permute(value, ring_links(downs, roots))
            value = value + up + down
        return value

    width = solved.shape[0]
    low = spread_ends(jnp.concatenate(held[:2], axis=0))
    first = low[width:]
    first = first + permute(first, neighbour_links(parts))
    second = spread_ends(held[2])
    second = second + permute(second, halving_links(parts, 2, 1))
    second = second + permute(second, neighbour_links(parts))
    low = spread_chips(jnp.concatenate([low[:width], first, second], axis=0))
    third = spread_ends(held[3])
    for bit in (2, 1):
        third = third + permute(third, halving_links(parts, 3, bit))
    third = third + permute(third, neighbour_links(parts))
    last = held[top]
    got = [permute(last, top_links(parts, [((0, LAST), to)])) for to in ((RING, 0), (RING, LAST), (0, 0))]
    last = spread_rings(last + got[0] + got[1] + got[2], (True, True, False, False))
    pair = spread_chips(jnp.concatenate([third, last], axis=0))

    def spread_update(out, level, full):
        return out - lax.dot_general(
            spikes[level], full, (((1,), (1,)), ((), ())), precision=MODE, preferred_element_type=jnp.float32
        )

    out = right_side
    for value, first in ((low, 0), (pair, 3)):
        count = value.shape[0] // width
        ends = cores_gather(value)
        for k in range(count):
            full = jnp.concatenate([ends[i * width : (i + 1) * width] for i in (k, k + count)], axis=0)
            out = spread_update(out, first + k, full)
    return out


def solution(mesh):
    fine = Mesh(mesh.devices.reshape(mesh.shape["dom"], CHIPS, CORES), AXES)
    rows = ("dom", "y", "c")
    in_specs = (P(rows, None), P(None, rows, None), P("dom", ("y", "c"), None))

    return jax.shard_map(body, mesh=fine, in_specs=in_specs, out_specs=P(rows, None), check_vma=False)
```
